32 devices in a mesh: row: 4 (over y, x), col: 8 (over z, core).
Axes of the slice: x: 2, y: 2, z: 4, core: 2. Of those that a mesh axis runs over, the one named last changes fastest.
Arguments:
- latents: bfloat16 [1, 32, 32, 8192], P(None, 'col', None, 'row'), may hold values from -6 to 6
- kernel: bfloat16 [3, 3, 8192, 8192], P(None, None, 'row', 'col'), may hold values from -0.0234375 to 0.0234375
- out_grad: bfloat16 [1, 32, 32, 8192], P(None, 'row', None, 'col'), may hold values from -6 to 6
Outputs:
- conv_out: bfloat16 [1, 32, 32, 8192], P(None, 'row', None, 'col')
- latent_grad: bfloat16 [1, 32, 32, 8192], P(None, 'col', None, 'row')
The draws below stay inside these ranges and needn't reach their ends.
All inputs are finite; a program needn't handle non-finite values.
Results may differ from the reference program's by a relative error of at most 0.001.
Values may be sent and summed in bfloat16 or wider, within the bound.
A program may use at most 192 MiB of HBM per device.

```python
import jax
import jax.numpy as jnp
from jax import lax

CIN = 8192
COUT = 8192
H = 32
W = 32
B = 1


def block_scale(stream_key, dims, shards, least, high):
    factor_of = 1.0
    for dim, blocks in shards:
        steps = jax.random.uniform(jax.random.fold_in(jax.random.fold_in(stream_key, 6), dim), (blocks,), jnp.float32, least / len(shards), high / len(shards))
        factor_of = factor_of * jnp.repeat(jnp.exp(steps), dims[dim] // blocks).reshape((-1,) + (1,) * (len(dims) - 1 - dim))
    return factor_of


def centred(rng, shape, deviation, bound, shards=(), kind=jnp.bfloat16):
    drawn = jax.random.normal(rng, shape, jnp.float32) * deviation
    if len(shards) > 0:
        drawn = block_scale(rng, shape, shards, -0.22, 0.18) * drawn
    return jnp.clip(drawn, min=-bound, max=bound).astype(kind)


def setup_inputs(seed: int = 0) -> dict:
    arg_keys = jax.random.split(jax.random.key(seed), 4)
    return {
        "latents": centred(arg_keys[0], (B, H, W, CIN), 1.0, 6.0, ((1, 8), (3, 4))),
        "kernel": centred(arg_keys[1], (3, 3, CIN, COUT), (9 * CIN) ** -0.5, 0.0234375, ((2, 4), (3, 8))),
        "out_grad": centred(arg_keys[2], (B, H, W, COUT), 1.0, 6.0, ((1, 4), (3, 8))),
    }


def reference(latents, kernel, out_grad):
    numbers = ("NHWC", "HWIO", "NHWC")
    forward = lax.conv_general_dilated(latents, kernel, (1, 1), "SAME", dimension_numbers=numbers, preferred_element_type=jnp.float32)
    flipped = jnp.transpose(kernel[::-1, ::-1], (0, 1, 3, 2))
    backward = lax.conv_general_dilated(out_grad, flipped, (1, 1), "SAME", dimension_numbers=numbers, preferred_element_type=jnp.float32)
    return forward.astype(jnp.bfloat16), backward.astype(jnp.bfloat16)
```

```python
import functools

import jax
import jax.numpy as jnp
from jax import lax
from jax.experimental import pallas as pl
from jax.experimental.pallas import tpu as pltpu
from jax.sharding import PartitionSpec as P

MESH = pl.DeviceIdType.MESH
SLOTS = 4


def dot_nn(a, b):
    return jnp.dot(a, b, preferred_element_type=jnp.float32)


def dot_nt(a, b):
    return lax.dot_general(a, b, (((1,), (1,)), ((), ())), preferred_element_type=jnp.float32)


def kernel(cfg, lat, ker, og, conv, lgrad, gpad, xpad, acc, wb, wf, bp, pr, zr, fp, fr,
           wbs, wfs, loc, ogs, ogr, las, lar, prs, prr, zrs, zrr, frs, frr):
    R, C, W, M, rw, cw, ci, co, tb, tf = cfg
    nb, nf, nz = ci // tb, co // tf, C // 2
    r = lax.axis_index("row")
    c = lax.axis_index("col")
    z, me = c // 2, c % 2
    other = 1 - me

    def fetch_b(s):
        t, kw, kh = s // 9, (s % 9) // 3, s % 3
        return pltpu.make_async_copy(
            ker.at[kh, kw, pl.ds(pl.multiple_of(t * tb, tb), tb), :], wb.at[s % SLOTS], wbs.at[s % SLOTS])

    def fetch_f(s):
        t, kw, kh = s // 9, (s % 9) // 3, s % 3
        return pltpu.make_async_copy(
            ker.at[kh, kw, :, pl.ds(pl.multiple_of(t * tf, tf), tf)], wf.at[s % SLOTS], wfs.at[s % SLOTS])

    for s in range(SLOTS - 1):
        fetch_b(s).start()
        fetch_f(s).start()

    def g_block(k):
        return gpad.at[pl.ds(pl.multiple_of(W + k * rw, W), rw), :]

    def x_block(k):
        return xpad.at[pl.ds(pl.multiple_of(W + k * cw, W), cw), :]

    own_g = pltpu.make_async_copy(og, g_block(r), loc.at[0])
    own_x = pltpu.make_async_copy(lat, x_block(c), loc.at[1])
    own_g.start()
    own_x.start()

    barrier = pltpu.get_barrier_semaphore()
    for d in range(1, R):
        pl.semaphore_signal(barrier, inc=1, device_id={"row": (r + d) % R}, device_id_type=MESH)
    for d in range(1, C):
        pl.semaphore_signal(barrier, inc=1, device_id={"col": (c + d) % C}, device_id_type=MESH)
    pl.semaphore_wait(barrier, R - 1 + C - 1)

    def send_g(d, k):
        return pltpu.make_async_remote_copy(
            src_ref=og, dst_ref=g_block(k), send_sem=ogs.at[d - 1], recv_sem=ogr.at[d - 1],
            device_id={"row": (r + d) % R}, device_id_type=MESH)

    def send_x(d, k):
        return pltpu.make_async_remote_copy(
            src_ref=lat, dst_ref=x_block(k), send_sem=las.at[d - 1], recv_sem=lar.at[d - 1],
            device_id={"col": (c + d) % C}, device_id_type=MESH)

    for d in range(1, R):
        send_g(d, r).start()
    for d in range(1, C):
        send_x(d, c).start()

    gpad[:W, :] = jnp.zeros((W, co), gpad.dtype)
    gpad[M + W :, :] = jnp.zeros((W, co), gpad.dtype)
    xpad[:W, :] = jnp.zeros((W, ci), xpad.dtype)
    xpad[M + W :, :] = jnp.zeros((W, ci), xpad.dtype)

    def send_pair(t):
        return pltpu.make_async_remote_copy(
            src_ref=bp.at[t, other], dst_ref=pr.at[t], send_sem=prs.at[t], recv_sem=prr.at[t],
            device_id={"col": z * 2 + other}, device_id_type=MESH)

    def send_z(t, d, slot):
        peer = (z + d) % nz
        return pltpu.make_async_remote_copy(
            src_ref=bp.at[t, me, peer], dst_ref=zr.at[t, slot], send_sem=zrs.at[t, d - 1],
            recv_sem=zrr.at[t, d - 1], device_id={"col": peer * 2 + me}, device_id_type=MESH)

    def send_r(t, d, slot):
        peer = (r + d) % R
        return pltpu.make_async_remote_copy(
            src_ref=fp.at[t, peer], dst_ref=fr.at[t, slot], send_sem=frs.at[t, d - 1],
            recv_sem=frr.at[t, d - 1], device_id={"row": peer}, device_id_type=MESH)

    def pair_sum(t):
        send_pair(t).wait_recv()

        def add(k, _):
            bp[t, me, k] = bp[t, me, k] + pr[t, k]
            return 0

        lax.fori_loop(0, nz, add, 0)
        for d in range(1, nz):
            send_z(t, d, z).start()

    def shifted(lo, n, first, last, cols):
        col = lax.broadcasted_iota(jnp.int32, (n, cols), 0) % W
        rows = pl.ds(pl.multiple_of(lo, n), n)
        down = pltpu.roll(acc[first, rows, :cols], 1, 0)
        up = pltpu.roll(acc[last, rows, :cols], n - 1, 0)
        return acc[1, rows, :cols] + jnp.where(col == 0, 0.0, down) + jnp.where(col == W - 1, 0.0, up)

    own_g.wait()
    for d in range(1, R):
        send_g(d, (r + R - d) % R).wait_recv()

    def taps(t, fetch, total, buf, dot, src, flip, cols):
        def step(kw, _):
            for kh in range(3):
                s = t * 9 + kw * 3 + kh
                fetch(s).wait()

                @pl.when(s + SLOTS - 1 < total)
                def _():
                    fetch(s + SLOTS - 1).start()

                top = (2 - kh) * W if flip else kh * W
                part = dot(src[top : top + M, :], buf[s % SLOTS])
                if kh == 0:
                    acc[kw, :, :cols] = part
                else:
                    acc[kw, :, :cols] += part
            return 0

        lax.fori_loop(0, 3, step, 0)

    def back(t, _):
        taps(t, fetch_b, nb * 9, wb, dot_nt, gpad, True, tb)

        def put(k, _):
            bp[t, k % 2, k // 2] = shifted(k * cw, cw, 2, 0, tb)
            return 0

        lax.fori_loop(0, C, put, 0)
        send_pair(t).start()

        @pl.when(t > 0)
        def _():
            pair_sum(t - 1)

        return 0

    lax.fori_loop(0, nb, back, 0)

    own_x.wait()
    for d in range(1, C):
        send_x(d, (c + C - d) % C).wait_recv()

    def fore(t, _):
        taps(t, fetch_f, nf * 9, wf, dot_nn, xpad, False, tf)

        def put(k, _):
            fp[t, k] = shifted(k * rw, rw, 0, 2, tf)
            return 0

        lax.fori_loop(0, R, put, 0)
        for d in range(1, R):
            send_r(t, d, r).start()

        @pl.when(t == 0)
        def _():
            pair_sum(nb - 1)

        return 0

    lax.fori_loop(0, nf, fore, 0)

    for d in range(1, R):
        send_g(d, r).wait_send()
    for d in range(1, C):
        send_x(d, c).wait_send()
    for t in range(nb):
        send_pair(t).wait_send()
        total = bp[t, me, z]
        for d in range(1, nz):
            src = (z + nz - d) % nz
            send_z(t, d, src).wait_recv()
            total = total + zr[t, src]
        lgrad[:, t * tb : (t + 1) * tb] = total.astype(lgrad.dtype)
        for d in range(1, nz):
            send_z(t, d, z).wait_send()
    for t in range(nf):
        total = fp[t, r]
        for d in range(1, R):
            src = (r + R - d) % R
            send_r(t, d, src).wait_recv()
            total = total + fr[t, src]
        conv[:, t * tf : (t + 1) * tf] = total.astype(conv.dtype)
        for d in range(1, R):
            send_r(t, d, r).wait_send()


def body(R, C, latents, kern, out_grad):
    _, hc, W, ci = latents.shape
    hr, co = out_grad.shape[1], out_grad.shape[3]
    M, rw, cw = hr * R * W, hr * W, hc * W
    tb, tf = min(512, ci), min(256, co)
    nb, nf, nz = ci // tb, co // tf, C // 2
    cfg = (R, C, W, M, rw, cw, ci, co, tb, tf)
    bf, f32 = jnp.bfloat16, jnp.float32
    dma = pltpu.SemaphoreType.DMA
    conv, lgrad = pl.pallas_call(
        functools.partial(kernel, cfg),
        out_shape=(jax.ShapeDtypeStruct((rw, co), bf), jax.ShapeDtypeStruct((cw, ci), bf)),
        in_specs=[pl.BlockSpec(memory_space=pl.ANY)] * 3,
        out_specs=(pl.BlockSpec(memory_space=pltpu.VMEM),) * 2,
        scratch_shapes=[
            pltpu.VMEM((M + 2 * W, co), bf),
            pltpu.VMEM((M + 2 * W, ci), bf),
            pltpu.VMEM((3, M, max(tb, tf)), f32),
            pltpu.VMEM((SLOTS, tb, co), bf),
            pltpu.VMEM((SLOTS, ci, tf), bf),
            pltpu.VMEM((nb, 2, nz, cw, tb), f32),
            pltpu.VMEM((nb, nz, cw, tb), f32),
            pltpu.VMEM((nb, nz, cw, tb), f32),
            pltpu.VMEM((nf, R, rw, tf), f32),
            pltpu.VMEM((nf, R, rw, tf), f32),
            dma((SLOTS,)), dma((SLOTS,)), dma((2,)),
            dma((R - 1,)), dma((R - 1,)),
            dma((C - 1,)), dma((C - 1,)),
            dma((nb,)), dma((nb,)),
            dma((nb, nz - 1)), dma((nb, nz - 1)),
            dma((nf, R - 1)), dma((nf, R - 1)),
        ],
        compiler_params=pltpu.CompilerParams(
            collective_id=0, has_side_effects=True, vmem_limit_bytes=66 * 1000 * 1000),
    )(latents.reshape(cw, ci), kern, out_grad.reshape(rw, co))
    return conv.reshape(1, hr, W, co), lgrad.reshape(1, hc, W, ci)


def solution(mesh):
    in_specs = (
        P(None, "col", None, "row"),
        P(None, None, "row", "col"),
        P(None, "row", None, "col"),
    )
    out_specs = (P(None, "row", None, "col"), P(None, "col", None, "row"))
    run = functools.partial(body, mesh.shape["row"], mesh.shape["col"])
    return jax.shard_map(run, mesh=mesh, in_specs=in_specs, out_specs=out_specs, check_vma=False)
```

```python
import functools

import jax
import jax.numpy as jnp
from jax import lax
from jax.experimental import pallas as pl
from jax.experimental.pallas import tpu as pltpu
from jax.sharding import PartitionSpec as P

MESH = pl.DeviceIdType.MESH
SLOTS = 6


def dot_nn(a, b):
    return jnp.dot(a, b, preferred_element_type=jnp.float32)


def dot_nt(a, b):
    return lax.dot_general(a, b, (((1,), (1,)), ((), ())), preferred_element_type=jnp.float32)


def kernel(cfg, lat, ker, og, conv, lgrad, gpad, xpad, acc, wb, wf, bp, pr, qr, zr, fp, fr,
           wbs, wfs, loc, ogs, ogr, las, lar, res, rer, prs, prr, qrs, qrr, zrs, zrr, frs, frr):
    R, C, W, M, rw, cw, ci, co, tb, tf = cfg
    nb, nf, nz = ci // tb, co // tf, C // 2
    nq = nz // 2
    r = lax.axis_index("row")
    c = lax.axis_index("col")
    z, me = c // 2, c % 2
    other = 1 - me
    q, zp = z // 2, z % 2
    mate = 1 - zp

    def fetch_b(s):
        t, kw, kh = s // 9, (s % 9) // 3, s % 3
        return pltpu.make_async_copy(
            ker.at[kh, kw, pl.ds(pl.multiple_of(t * tb, tb), tb), :], wb.at[s % SLOTS], wbs.at[s % SLOTS])

    def fetch_f(s):
        t, kw, kh = s // 9, (s % 9) // 3, s % 3
        return pltpu.make_async_copy(
            ker.at[kh, kw, :, pl.ds(pl.multiple_of(t * tf, tf), tf)], wf.at[s % SLOTS], wfs.at[s % SLOTS])

    for s in range(3):
        fetch_b(s).start()
        fetch_f(s).start()

    def g_block(k):
        return gpad.at[pl.ds(pl.multiple_of(W + k * rw, W), rw), :]

    def x_block(k):
        return xpad.at[pl.ds(pl.multiple_of(W + k * cw, W), cw), :]

    own_g = pltpu.make_async_copy(og, g_block(r), loc.at[0])
    own_x = pltpu.make_async_copy(lat, x_block(c), loc.at[1])
    own_g.start()
    own_x.start()

    barrier = pltpu.get_barrier_semaphore()
    for d in range(1, R):
        pl.semaphore_signal(barrier, inc=1, device_id={"row": (r + d) % R}, device_id_type=MESH)
    for d in range(1, nz):
        pl.semaphore_signal(barrier, inc=1, device_id={"col": (z + d) % nz * 2 + me}, device_id_type=MESH)
    pl.semaphore_signal(barrier, inc=1, device_id={"col": z * 2 + other}, device_id_type=MESH)
    pl.semaphore_wait(barrier, R - 1 + nz)

    def send_g(d, k):
        return pltpu.make_async_remote_copy(
            src_ref=og, dst_ref=g_block(k), send_sem=ogs.at[d - 1], recv_sem=ogr.at[d - 1],
            device_id={"row": (r + d) % R}, device_id_type=MESH)

    def send_x(d, k):
        peer = z * 2 + other if d == 0 else (z + d) % nz * 2 + me
        return pltpu.make_async_remote_copy(
            src_ref=lat, dst_ref=x_block(k), send_sem=las.at[d], recv_sem=lar.at[d],
            device_id={"col": peer}, device_id_type=MESH)

    def relay_x(d, core):
        k = (z + nz - d) % nz * 2 + core
        return pltpu.make_async_remote_copy(
            src_ref=x_block(k), dst_ref=x_block(k), send_sem=res.at[d - 1], recv_sem=rer.at[d - 1],
            device_id={"col": z * 2 + other}, device_id_type=MESH)

    for d in range(1, R):
        send_g(d, r).start()
    for d in range(nz - 1, -1, -1):
        send_x(d, c).start()

    gpad[:W, :] = jnp.zeros((W, co), gpad.dtype)
    gpad[M + W :, :] = jnp.zeros((W, co), gpad.dtype)
    xpad[:W, :] = jnp.zeros((W, ci), xpad.dtype)
    xpad[M + W :, :] = jnp.zeros((W, ci), xpad.dtype)

    def send_pair(t):
        return pltpu.make_async_remote_copy(
            src_ref=bp.at[t, other], dst_ref=pr.at[t], send_sem=prs.at[t], recv_sem=prr.at[t],
            device_id={"col": z * 2 + other}, device_id_type=MESH)

    def send_mate(t):
        return pltpu.make_async_remote_copy(
            src_ref=bp.at[t, me, mate], dst_ref=qr.at[t], send_sem=qrs.at[t], recv_sem=qrr.at[t],
            device_id={"col": (q * 2 + mate) * 2 + me}, device_id_type=MESH)

    def send_z(t, d, slot):
        peer = (q + d) % nq
        return pltpu.make_async_remote_copy(
            src_ref=bp.at[t, me, zp, peer], dst_ref=zr.at[t, slot], send_sem=zrs.at[t, d - 1],
            recv_sem=zrr.at[t, d - 1], device_id={"col": (peer * 2 + zp) * 2 + me}, device_id_type=MESH)

    def send_r(t, d, slot):
        peer = (r + d) % R
        return pltpu.make_async_remote_copy(
            src_ref=fp.at[t, peer], dst_ref=fr.at[t, slot], send_sem=frs.at[t, d - 1],
            recv_sem=frr.at[t, d - 1], device_id={"row": peer}, device_id_type=MESH)

    def pair_sum(t):
        send_pair(t).wait_recv()

        def add(k, _):
            bp[t, me, k // nq, k % nq] = bp[t, me, k // nq, k % nq] + pr[t, k // nq, k % nq]
            return 0

        lax.fori_loop(0, nz, add, 0)
        send_mate(t).start()

    def mate_sum(t):
        send_mate(t).wait_recv()

        def add(k, _):
            bp[t, me, zp, k] = bp[t, me, zp, k] + qr[t, k]
            return 0

        lax.fori_loop(0, nq, add, 0)
        for d in range(1, nq):
            send_z(t, d, q).start()

    def advance(i):
        @pl.when((i >= 1) & (i <= nb))
        def _():
            pair_sum(i - 1)

        @pl.when((i >= 3) & (i <= nb + 2))
        def _():
            mate_sum(i - 3)

    def shifted(lo, n, first, last, cols):
        col = lax.broadcasted_iota(jnp.int32, (n, cols), 0) % W
        rows = pl.ds(pl.multiple_of(lo, n), n)
        down = pltpu.roll(acc[first, rows, :cols], 1, 0)
        up = pltpu.roll(acc[last, rows, :cols], n - 1, 0)
        return acc[1, rows, :cols] + jnp.where(col == 0, 0.0, down) + jnp.where(col == W - 1, 0.0, up)

    own_g.wait()
    for d in range(1, R):
        send_g(d, (r + R - d) % R).wait_recv()

    def taps(t, fetch, total, buf, dot, src, flip, cols):
        def step(kw, _):
            s0 = t * 9 + kw * 3

            @pl.when(s0 + 3 < total)
            def _():
                for kh in range(3):
                    fetch(s0 + 3 + kh).start()

            part = None
            for kh in range(3):
                fetch(s0 + kh).wait()
            for kh in range(3):
                top = (2 - kh) * W if flip else kh * W
                term = dot(src[top : top + M, :], buf[(s0 + kh) % SLOTS])
                part = term if part is None else part + term
            acc[kw, :, :cols] = part
            return 0

        lax.fori_loop(0, 3, step, 0)

    def back(t, _):
        taps(t, fetch_b, nb * 9, wb, dot_nt, gpad, True, tb)

        def put(k, _):
            bp[t, k % 2, k // 2 % 2, k // 4] = shifted(k * cw, cw, 2, 0, tb)
            return 0

        lax.fori_loop(0, C, put, 0)
        send_pair(t).start()

        advance(t)

        @pl.when(t == max(nb - 2, 0))
        def _():
            for d in range(1, nz):
                k = (z + nz - d) % nz * 2 + me
                send_x(d, k).wait_recv()
                relay_x(d, me).start()

        return 0

    lax.fori_loop(0, nb, back, 0)

    own_x.wait()
    send_x(0, z * 2 + other).wait_recv()
    for d in range(1, nz):
        relay_x(d, other).wait_recv()

    def fore(t, _):
        taps(t, fetch_f, nf * 9, wf, dot_nn, xpad, False, tf)

        def put(k, _):
            fp[t, k] = shifted(k * rw, rw, 0, 2, tf)
            return 0

        lax.fori_loop(0, R, put, 0)
        for d in range(1, R):
            send_r(t, d, r).start()

        advance(nb + t)
        return 0

    lax.fori_loop(0, nf, fore, 0)

    for d in range(1, R):
        send_g(d, r).wait_send()
    for i in range(nb + nf, nb + 3):
        if i <= nb:
            pair_sum(i - 1)
        if i >= 3:
            mate_sum(i - 3)
    for d in range(nz):
        send_x(d, c).wait_send()
    for d in range(1, nz):
        relay_x(d, me).wait_send()
    for t in range(nb):
        send_pair(t).wait_send()
        send_mate(t).wait_send()
        total = bp[t, me, zp, q]
        for d in range(1, nq):
            src = (q + nq - d) % nq
            send_z(t, d, src).wait_recv()
            total = total + zr[t, src]
        lgrad[:, t * tb : (t + 1) * tb] = total.astype(lgrad.dtype)
        for d in range(1, nq):
            send_z(t, d, q).wait_send()
    for t in range(nf):
        total = fp[t, r]
        for d in range(1, R):
            src = (r + R - d) % R
            send_r(t, d, src).wait_recv()
            total = total + fr[t, src]
        conv[:, t * tf : (t + 1) * tf] = total.astype(conv.dtype)
        for d in range(1, R):
            send_r(t, d, r).wait_send()


def body(R, C, latents, kern, out_grad):
    _, hc, W, ci = latents.shape
    hr, co = out_grad.shape[1], out_grad.shape[3]
    M, rw, cw = hr * R * W, hr * W, hc * W
    tb, tf = min(512, ci), min(256, co)
    nb, nf, nz = ci // tb, co // tf, C // 2
    nq = nz // 2
    cfg = (R, C, W, M, rw, cw, ci, co, tb, tf)
    bf, f32 = jnp.bfloat16, jnp.float32
    dma = pltpu.SemaphoreType.DMA
    conv, lgrad = pl.pallas_call(
        functools.partial(kernel, cfg),
        out_shape=(jax.ShapeDtypeStruct((rw, co), bf), jax.ShapeDtypeStruct((cw, ci), bf)),
        in_specs=[pl.BlockSpec(memory_space=pl.ANY)] * 3,
        out_specs=(pl.BlockSpec(memory_space=pltpu.VMEM),) * 2,
        scratch_shapes=[
            pltpu.VMEM((M + 2 * W, co), bf),
            pltpu.VMEM((M + 2 * W, ci), bf),
            pltpu.VMEM((3, M, max(tb, tf)), f32),
            pltpu.VMEM((SLOTS, tb, co), bf),
            pltpu.VMEM((SLOTS, ci, tf), bf),
            pltpu.VMEM((nb, 2, 2, nq, cw, tb), f32),
            pltpu.VMEM((nb, 2, nq, cw, tb), f32),
            pltpu.VMEM((nb, nq, cw, tb), f32),
            pltpu.VMEM((nb, nq, cw, tb), f32),
            pltpu.VMEM((nf, R, rw, tf), f32),
            pltpu.VMEM((nf, R, rw, tf), f32),
            dma((SLOTS,)), dma((SLOTS,)), dma((2,)),
            dma((R - 1,)), dma((R - 1,)),
            dma((nz,)), dma((nz,)), dma((nz - 1,)), dma((nz - 1,)),
            dma((nb,)), dma((nb,)), dma((nb,)), dma((nb,)),
            dma((nb, nq - 1)), dma((nb, nq - 1)),
            dma((nf, R - 1)), dma((nf, R - 1)),
        ],
        compiler_params=pltpu.CompilerParams(
            collective_id=0, has_side_effects=True, vmem_limit_bytes=66 * 1000 * 1000),
    )(latents.reshape(cw, ci), kern, out_grad.reshape(rw, co))
    return conv.reshape(1, hr, W, co), lgrad.reshape(1, hc, W, ci)


def solution(mesh):
    in_specs = (
        P(None, "col", None, "row"),
        P(None, None, "row", "col"),
        P(None, "row", None, "col"),
    )
    out_specs = (P(None, "row", None, "col"), P(None, "col", None, "row"))
    run = functools.partial(body, mesh.shape["row"], mesh.shape["col"])
    return jax.shard_map(run, mesh=mesh, in_specs=in_specs, out_specs=out_specs, check_vma=False)
```
